32 devices in a mesh: groups: 2 (over y), tok: 16 (over z, x, core).
Axes of the slice: x: 2, y: 2, z: 4, core: 2. Of those that a mesh axis runs over, the one named last changes fastest.
Arguments:
- query_rows: bfloat16 [8192, 768], P(('groups', 'tok')), parts along dimension 0, may hold values from -6 to 6
- key_rows: bfloat16 [8192, 768], P(('groups', 'tok')), parts along dimension 0, may hold values from -6 to 6
- value_rows: bfloat16 [8192, 768], P(('groups', 'tok')), parts along dimension 0, may hold values from -6 to 6
- out_rows: bfloat16 [8192, 768], P(('groups', 'tok')), parts along dimension 0, may hold values from -6 to 6
- grad_out: bfloat16 [8192, 768], P(('groups', 'tok')), parts along dimension 0, may hold values from -6 to 6
- normalizer: float32 [16, 8192], P(None, ('groups', 'tok')), parts along dimension 1, may hold values from 3 to 5
- keep_tasks: int32 [32, 5], P('groups'), parts along dimension 0, may hold values from 0 to 1, as said below
Outputs:
- grad_query: bfloat16 [8192, 768], P(('groups', 'tok')), parts along dimension 0
- grad_key: bfloat16 [8192, 768], P(('groups', 'tok')), parts along dimension 0
- grad_value: bfloat16 [8192, 768], P(('groups', 'tok')), parts along dimension 0
The draws below stay inside these ranges and needn't reach their ends.
There are 2 independent parts, one for each index of `groups`. The reference program is written for one: setup_inputs(seed, part) draws one part's arguments, and reference() takes and returns one part's arrays. A program takes and returns all parts, laid end to end along the dimension named above; each array names one. Nothing has to cross between parts.
Inputs may be any that keep to these rules, and one draw needn't show every extreme that they name: keep_tasks[a, 2] = 1 for every block a; entries naming a key block outside 0 to 15 are ignored.
All inputs are finite; a program needn't handle non-finite values.
Results may differ from the reference program's by a relative error of at most 0.0053.
Values may be sent and summed in bfloat16 or wider, within the bound.
A program may use at most 128 MiB of HBM per device.

```python
import jax
import jax.numpy as jnp
from jax import lax

D = 768
HEADS = 16
BLOCK = 256
RADIUS = 2
WIN = 5
NBLK = 16
TOKENS = 4096


def draw_keep_tasks(key, part):
    first = jax.random.fold_in(key, 11)
    second = jax.random.fold_in(key, 23)
    density = jax.random.randint(first, (NBLK, 1), 0, 5)
    levels = jax.random.randint(second, (NBLK, WIN), 0, 4)
    column = jnp.arange(WIN)[None, :]
    keep = (levels < density) | (column == RADIUS)
    return jnp.where(keep, 1, 0).astype(jnp.int32)


def steps_of(own_key, dims, pieces, smallest, top_value):
    def one(axis_at, parts):
        heights = jax.random.uniform(jax.random.fold_in(jax.random.fold_in(own_key, 6), axis_at), (parts,), jnp.float32, smallest / len(pieces), top_value / len(pieces))
        return jnp.repeat(jnp.exp(heights), dims[axis_at] // parts).reshape((-1,) + (1,) * (len(dims) - axis_at - 1))

    gain = one(*pieces[0])
    for cut in pieces[1:]:
        gain = gain * one(*cut)
    return gain


def centred(rng, extent, spread, bound, shards=(), held_as=jnp.bfloat16):
    array = jax.random.normal(rng, extent, jnp.float32) * spread
    if len(shards) > 0:
        array = steps_of(rng, extent, shards, -0.22, 0.18) * array
    return jnp.clip(array, min=-bound, max=bound).astype(held_as)


def setup_inputs(seed: int = 0, part: int = 0) -> dict:
    key_list = jax.random.split(jax.random.key(seed), 8)
    own_keys = jax.random.split(jax.random.fold_in(key_list[7], part), 8)
    query_rows = centred(own_keys[0], (TOKENS, D), 1.0, 6.0, ((0, 16),))
    key_rows = centred(own_keys[1], (TOKENS, D), 1.0, 6.0, ((0, 16),))
    value_rows = centred(own_keys[2], (TOKENS, D), 1.0, 6.0, ((0, 16),))
    out_rows = centred(own_keys[3], (TOKENS, D), 1.0, 6.0, ((0, 16),))
    grad_out = centred(own_keys[4], (TOKENS, D), 1.0, 6.0, ((0, 16),))
    normalizer = jnp.clip(3.0 + 2.0 * jax.random.uniform(own_keys[5], (HEADS, TOKENS), jnp.float32) ** steps_of(own_keys[5], (HEADS, TOKENS), ((1, 16),), -0.2, 0.2), 3.0, 5.0)
    keep_tasks = draw_keep_tasks(jax.random.fold_in(jax.random.fold_in(key_list[7], part), 71), part)
    return dict(query_rows=query_rows, key_rows=key_rows, value_rows=value_rows, out_rows=out_rows, grad_out=grad_out, normalizer=normalizer, keep_tasks=keep_tasks)


def task_grads(q_block, dout_block, lse_block, delta_block, k_block, v_block, scale):
    scores = jnp.einsum('qhe,khe->hqk', q_block, k_block) * scale
    probs = jnp.exp(scores - lse_block[:, :, None])
    prob_grad = jnp.einsum('qhe,khe->hqk', dout_block, v_block)
    score_grad = lax.optimization_barrier((probs * (prob_grad - delta_block[:, :, None])).astype(jnp.bfloat16)).astype(jnp.float32)
    probs_low = lax.optimization_barrier(probs.astype(jnp.bfloat16)).astype(jnp.float32)
    term_q = jnp.einsum('hqk,khe->qhe', score_grad, k_block) * scale
    term_k = jnp.einsum('hqk,qhe->khe', score_grad, q_block) * scale
    term_v = jnp.einsum('hqk,qhe->khe', probs_low, dout_block)
    return term_q, term_k, term_v


def reference(query_rows, key_rows, value_rows, out_rows, grad_out, normalizer, keep_tasks):
    width = query_rows.shape[1]
    head_dim = width // HEADS
    scale = head_dim ** -0.5
    shape4 = (NBLK, BLOCK, HEADS, head_dim)
    q_all = query_rows.astype(jnp.float32).reshape(shape4)
    k_all = key_rows.astype(jnp.float32).reshape(shape4)
    v_all = value_rows.astype(jnp.float32).reshape(shape4)
    o_all = out_rows.astype(jnp.float32).reshape(shape4)
    g_all = grad_out.astype(jnp.float32).reshape(shape4)
    delta = jnp.transpose(jnp.sum(g_all * o_all, axis=3), (0, 2, 1))
    lse_all = jnp.transpose(normalizer.astype(jnp.float32).reshape(HEADS, NBLK, BLOCK), (1, 0, 2))
    padding = jnp.zeros((RADIUS, BLOCK, HEADS, head_dim), jnp.float32)
    k_pad = jnp.concatenate([padding, k_all, padding], axis=0)
    v_pad = jnp.concatenate([padding, v_all, padding], axis=0)
    zeros3 = jnp.zeros((BLOCK, HEADS, head_dim), jnp.float32)

    def step(carry, block):
        dk_pad, dv_pad = carry
        q_block = lax.dynamic_index_in_dim(q_all, block, 0, keepdims=False)
        g_block = lax.dynamic_index_in_dim(g_all, block, 0, keepdims=False)
        lse_block = lax.dynamic_index_in_dim(lse_all, block, 0, keepdims=False)
        d_block = lax.dynamic_index_in_dim(delta, block, 0, keepdims=False)
        dq = zeros3
        for j in range(WIN):
            target = block - RADIUS + j
            inside = (target >= 0) & (target < NBLK)
            flag = jnp.where(inside, keep_tasks[block, j], 0)
            slot = (block + j).astype(jnp.int32)
            k_block = lax.dynamic_index_in_dim(k_pad, slot, 0, keepdims=False)
            v_block = lax.dynamic_index_in_dim(v_pad, slot, 0, keepdims=False)

            def live(unused):
                return task_grads(q_block, g_block, lse_block, d_block, k_block, v_block, scale)

            def dead(unused):
                return zeros3, zeros3, zeros3

            term_q, term_k, term_v = lax.cond(flag > 0, live, dead, 0)
            dq = dq + term_q
            old_k = lax.dynamic_index_in_dim(dk_pad, slot, 0, keepdims=False)
            dk_pad = lax.dynamic_update_index_in_dim(dk_pad, old_k + term_k, slot, 0)
            old_v = lax.dynamic_index_in_dim(dv_pad, slot, 0, keepdims=False)
            dv_pad = lax.dynamic_update_index_in_dim(dv_pad, old_v + term_v, slot, 0)
        return (dk_pad, dv_pad), dq

    start = (jnp.zeros_like(k_pad), jnp.zeros_like(v_pad))
    (dk_pad, dv_pad), dq_all = lax.scan(step, start, jnp.arange(NBLK, dtype=jnp.int32))
    total = NBLK * BLOCK
    grad_query = dq_all.reshape(total, width).astype(jnp.bfloat16)
    grad_key = dk_pad[RADIUS:RADIUS + NBLK].reshape(total, width).astype(jnp.bfloat16)
    grad_value = dv_pad[RADIUS:RADIUS + NBLK].reshape(total, width).astype(jnp.bfloat16)
    return grad_query, grad_key, grad_value
```

```python
import functools

import jax
import jax.numpy as jnp
from jax import lax
from jax.experimental import pallas as pl
from jax.experimental.pallas import tpu as pltpu
from jax.sharding import PartitionSpec as P

HEADS = 16
ROW = 4
PER = HEADS // ROW
LOG2E = 1.4426950408889634
MESH = pl.DeviceIdType.MESH
F32 = jnp.float32
BF16 = jnp.bfloat16


def dot_nn(a, b):
    return lax.dot_general(a, b, (((1,), (0,)), ((), ())), preferred_element_type=F32)


def dot_nt(a, b):
    return lax.dot_general(a, b, (((1,), (1,)), ((), ())), preferred_element_type=F32)


def kernel(
    count, q_ref, k_ref, v_ref, o_ref, g_ref, lse_ref, keep_ref,
    dq_out, dk_out, dv_out,
    kown, qown, sown, kbuf, qbuf, sbuf, dq, dkv, dqs, dqr, obuf, orecv,
    ks, kr, qs, qr, ss, sr, zs, zr, zss, zsr, ds, dr, os, orr,
):
    tok = lax.axis_index("tok")
    row, me = tok // ROW, tok % ROW
    rows = count // ROW
    has_low, has_high = row > 0, row < rows - 1
    width = q_ref.shape[1]
    dim = width // HEADS
    scale = dim ** -0.5

    barrier = pltpu.get_barrier_semaphore()

    def greet(target):
        pl.semaphore_signal(barrier, inc=1, device_id={"tok": target}, device_id_type=MESH)

    def mate(d):
        return row * ROW + (me + d) % ROW

    for d in range(1, ROW):
        greet(mate(d))

    @pl.when(has_low)
    def _():
        greet(tok - ROW)

    @pl.when(has_high)
    def _():
        greet(tok + ROW)

    def flipped(ref):
        return ref[...].T.reshape(HEADS, dim, ref.shape[0])

    qown[:, 0] = flipped(q_ref)
    g_t = flipped(g_ref)
    qown[:, 1] = g_t
    kown[:, 0] = flipped(k_ref)
    kown[:, 1] = flipped(v_ref)
    delta = jnp.sum(g_t.astype(F32) * flipped(o_ref).astype(F32), axis=1)
    lse2 = lse_ref[...] * LOG2E
    for j in range(ROW):
        sown[j, 0:PER] = lse2[j * PER:(j + 1) * PER]
        sown[j, PER:2 * PER] = delta[j * PER:(j + 1) * PER]

    pl.semaphore_wait(barrier, ROW - 1 + has_low.astype(jnp.int32) + has_high.astype(jnp.int32))

    def remote(src, dst, send, recv, target):
        return pltpu.make_async_remote_copy(
            src_ref=src, dst_ref=dst, send_sem=send, recv_sem=recv,
            device_id={"tok": target}, device_id_type=MESH,
        )

    def x_stat(d):
        to = (me + d) % ROW
        return remote(sown.at[to], sbuf.at[me + 2], ss.at[d], sr.at[d], mate(d))

    def x_q(d, h):
        to = (me + d) % ROW
        return remote(qown.at[to * PER + h], qbuf.at[me + 2, h], qs.at[d, h], qr.at[d, h], mate(d))

    def x_k(d, h):
        to = (me + d) % ROW
        return remote(kown.at[to * PER + h], kbuf.at[me, h], ks.at[d, h], kr.at[d, h], mate(d))

    def x_q_in(d, h):
        fr = (me + ROW - d) % ROW
        return remote(qown.at[0], qbuf.at[fr + 2, h], qs.at[d, h], qr.at[d, h], mate(d))

    def x_k_in(d, h):
        fr = (me + ROW - d) % ROW
        return remote(kown.at[0], kbuf.at[fr, h], ks.at[d, h], kr.at[d, h], mate(d))

    def x_stat_in(d):
        fr = (me + ROW - d) % ROW
        return remote(sown.at[0], sbuf.at[fr + 2], ss.at[d], sr.at[d], mate(d))

    order = (2, 1, 3)
    for d in order:
        x_stat(d).start()

    @pl.loop(0, PER)
    def _(h):
        for d in order:
            x_q(d, h).start()
        for d in order:
            x_k(d, h).start()

    @pl.loop(0, PER)
    def _(h):
        qbuf[me + 2, h] = qown[me * PER + h]
        kbuf[me, h] = kown[me * PER + h]

    sbuf[me + 2] = sown[me]

    @pl.when(jnp.logical_not(has_low))
    def _():
        dqr[0] = jnp.zeros(dqr.shape[1:], BF16)

    @pl.when(jnp.logical_not(has_high))
    def _():
        dqr[1] = jnp.zeros(dqr.shape[1:], BF16)

    def z_q(side, h):
        first, there = (2, 6) if side == 0 else (4, 0)
        target = tok - ROW if side == 0 else tok + ROW
        return remote(qbuf.at[pl.ds(first, 2), h], qbuf.at[pl.ds(there, 2), h],
                      zs.at[side, h], zr.at[1 - side, h], target)

    def z_q_in(side, h):
        here = 0 if side == 0 else 6
        target = tok - ROW if side == 0 else tok + ROW
        return remote(qbuf.at[pl.ds(here, 2), h], qbuf.at[pl.ds(here, 2), h],
                      zs.at[side, h], zr.at[side, h], target)

    def z_stat(side):
        first, there = (2, 6) if side == 0 else (4, 0)
        target = tok - ROW if side == 0 else tok + ROW
        return remote(sbuf.at[pl.ds(first, 2)], sbuf.at[pl.ds(there, 2)],
                      zss.at[side], zsr.at[1 - side], target)

    def z_stat_in(side):
        here = 0 if side == 0 else 6
        target = tok - ROW if side == 0 else tok + ROW
        return remote(sbuf.at[pl.ds(here, 2)], sbuf.at[pl.ds(here, 2)],
                      zss.at[side], zsr.at[side], target)

    def z_dq(side, h):
        target = tok - ROW if side == 0 else tok + ROW
        return remote(dqs.at[side, h], dqr.at[1 - side, h],
                      ds.at[side, h], dr.at[1 - side, h], target)

    def z_dq_in(side, h):
        target = tok - ROW if side == 0 else tok + ROW
        return remote(dqs.at[side, h], dqr.at[side, h],
                      ds.at[side, h], dr.at[side, h], target)

    def o_out(b, h):
        d = (b - me + ROW) % ROW
        return remote(obuf.at[b, h], orecv.at[me * PER + h],
                      os.at[d, h], orr.at[d, h], row * ROW + b)

    def o_in(d, h):
        fr = (me + ROW - d) % ROW
        return remote(obuf.at[0, h], orecv.at[fr * PER + h],
                      os.at[d, h], orr.at[d, h], mate(d))

    sides = ((0, has_low), (1, has_high))

    def sided(fn):
        for side, there in sides:
            @pl.when(there)
            def _():
                fn(side)

    for d in order:
        x_stat_in(d).wait_recv()
    sided(lambda side: z_stat(side).start())

    def task(c, slot, h, keys, values, keys_t):
        block = row * ROW + (slot - 2)
        flag = keep_ref[block, c + 4 - slot]
        gone = (1 - flag).astype(F32) * 1e30
        q_t, g_t = qbuf[slot, h, 0], qbuf[slot, h, 1]
        lse = sbuf[slot, pl.ds(h, 1), :] + gone
        delta = sbuf[slot, pl.ds(h + PER, 1), :]
        probs = jnp.exp2(dot_nn(keys, q_t) * (scale * LOG2E) - lse)
        grad = (probs * (dot_nn(values, g_t) - delta)).astype(BF16)
        return (
            dot_nn(keys_t, grad),
            dot_nt(q_t, grad),
            dot_nt(g_t, probs.astype(BF16)),
        )

    def run(h, work):
        seen = set()
        for c, slots, fresh in work:
            keys_t = kbuf[c, h, 0]
            keys = keys_t.T
            values = kbuf[c, h, 1].T
            dk = dv = None
            for slot in slots:
                tq, tk, tv = task(c, slot, h, keys, values, keys_t)
                dk = tk if dk is None else dk + tk
                dv = tv if dv is None else dv + tv
                if slot in seen:
                    dq[h, slot] += tq
                else:
                    dq[h, slot] = tq
                    seen.add(slot)
            if fresh:
                dkv[h, c, 0] = dk
                dkv[h, c, 1] = dv
            else:
                dkv[h, c, 0] += dk
                dkv[h, c, 1] += dv

    inner = ((0, (2, 3, 4), True), (1, (2, 3, 4, 5), True), (2, (2, 3, 4, 5), True), (3, (3, 4, 5), True))
    outer = (
        ((0, (0, 1), False), (1, (1,), False)),
        ((2, (6,), False), (3, (6, 7), False)),
    )

    def halo(side, h):
        z_q_in(side, h).wait_recv()
        run(h, outer[side])
        first = 0 if side == 0 else 6
        dqs[side, h] = (dq[h, pl.ds(first, 2)] * scale).astype(BF16)
        z_dq(side, h).start()

    def finish(h):
        sided(lambda side: z_dq_in(side, h).wait_recv())
        for b in range(ROW):
            total = dq[h, b + 2] * scale + dqr[b // 2, h, b % 2].astype(F32)
            obuf[b, h, 0] = total.astype(BF16)
            obuf[b, h, 1] = (dkv[h, b, 0] * scale).astype(BF16)
            obuf[b, h, 2] = dkv[h, b, 1].astype(BF16)

            @pl.when(b != me)
            def _():
                o_out(b, h).start()

            @pl.when(b == me)
            def _():
                orecv[me * PER + h] = obuf[b, h]

    @pl.loop(0, PER)
    def _(h):
        for d in order:
            x_q_in(d, h).wait_recv()
        sided(lambda side: z_q(side, h).start())
        for d in order:
            x_k_in(d, h).wait_recv()
        run(h, inner)

        @pl.when(h > 0)
        def _():
            finish(h - 1)

        @pl.when(h == 0)
        def _():
            sided(lambda side: z_stat_in(side).wait_recv())

        sided(lambda side: halo(side, h))

    finish(PER - 1)

    for d in order:
        x_stat(d).wait_send()
    sided(lambda side: z_stat(side).wait_send())

    @pl.loop(0, PER)
    def _(h):
        for d in order:
            x_q(d, h).wait_send()
            x_k(d, h).wait_send()
            o_in(d, h).wait_send()
            o_in(d, h).wait_recv()
        sided(lambda side: z_q(side, h).wait_send())
        sided(lambda side: z_dq(side, h).wait_send())

    for i, out in enumerate((dq_out, dk_out, dv_out)):
        out[...] = orecv[:, i].reshape(width, out.shape[0]).T


def per_device(count, query_rows, key_rows, value_rows, out_rows, grad_out, normalizer, keep_tasks):
    block, width = query_rows.shape
    dim = width // HEADS
    vmem = pl.BlockSpec(memory_space=pltpu.VMEM)
    dma = pltpu.SemaphoreType.DMA
    return pl.pallas_call(
        functools.partial(kernel, count),
        out_shape=[jax.ShapeDtypeStruct((block, width), BF16)] * 3,
        in_specs=[vmem] * 6 + [pl.BlockSpec(memory_space=pltpu.SMEM)],
        out_specs=[vmem] * 3,
        scratch_shapes=[
            pltpu.VMEM((HEADS, 2, dim, block), BF16),
            pltpu.VMEM((HEADS, 2, dim, block), BF16),
            pltpu.VMEM((ROW, 2 * PER, block), F32),
            pltpu.VMEM((ROW, PER, 2, dim, block), BF16),
            pltpu.VMEM((ROW + 4, PER, 2, dim, block), BF16),
            pltpu.VMEM((ROW + 4, 2 * PER, block), F32),
            pltpu.VMEM((PER, ROW + 4, dim, block), F32),
            pltpu.VMEM((PER, ROW, 2, dim, block), F32),
            pltpu.VMEM((2, PER, 2, dim, block), BF16),
            pltpu.VMEM((2, PER, 2, dim, block), BF16),
            pltpu.VMEM((ROW, PER, 3, dim, block), BF16),
            pltpu.VMEM((HEADS, 3, dim, block), BF16),
            dma((ROW, PER)), dma((ROW, PER)),
            dma((ROW, PER)), dma((ROW, PER)),
            dma((ROW,)), dma((ROW,)),
            dma((2, PER)), dma((2, PER)),
            dma((2,)), dma((2,)),
            dma((2, PER)), dma((2, PER)),
            dma((ROW, PER)), dma((ROW, PER)),
        ],
        compiler_params=pltpu.CompilerParams(
            collective_id=0, has_side_effects=True, vmem_limit_bytes=60 * 1024 * 1024
        ),
    )(query_rows, key_rows, value_rows, out_rows, grad_out, normalizer, keep_tasks)


def solution(mesh):
    rows = P(("groups", "tok"), None)
    return jax.shard_map(
        functools.partial(per_device, mesh.shape["tok"]),
        mesh=mesh,
        in_specs=(rows,) * 5 + (P(None, ("groups", "tok")), P("groups", None)),
        out_specs=(rows,) * 3,
        check_vma=False,
    )
```

```python
import functools

import jax
import jax.numpy as jnp
from jax import lax
from jax.experimental import pallas as pl
from jax.experimental.pallas import tpu as pltpu
from jax.sharding import PartitionSpec as P

HEADS = 16
ROW = 4
PER = HEADS // ROW
LOG2E = 1.4426950408889634
MESH = pl.DeviceIdType.MESH
F32 = jnp.float32
BF16 = jnp.bfloat16


def dot_nn(a, b):
    return lax.dot_general(a, b, (((1,), (0,)), ((), ())), preferred_element_type=F32)


def dot_nt(a, b):
    return lax.dot_general(a, b, (((1,), (1,)), ((), ())), preferred_element_type=F32)


def kernel(
    count, q_ref, k_ref, v_ref, o_ref, g_ref, lse_ref, keep_ref,
    orecv,
    kown, qown, sown, kbuf, qbuf, sbuf, dq, dkv, dqs, dqr, obuf,
    ks, kr, qs, qr, ss, sr, zs, zr, zss, zsr, ds, dr, os, orr,
):
    tok = lax.axis_index("tok")
    row, me = tok // ROW, tok % ROW
    rows = count // ROW
    has_low, has_high = row > 0, row < rows - 1
    width = q_ref.shape[1]
    dim = width // HEADS
    scale = dim ** -0.5

    barrier = pltpu.get_barrier_semaphore()

    def greet(target):
        pl.semaphore_signal(barrier, inc=1, device_id={"tok": target}, device_id_type=MESH)

    def mate(d):
        return row * ROW + (me + d) % ROW

    for d in range(1, ROW):
        greet(mate(d))

    @pl.when(has_low)
    def _():
        greet(tok - ROW)

    @pl.when(has_high)
    def _():
        greet(tok + ROW)

    def flipped(ref):
        return ref[...].T.reshape(HEADS, dim, ref.shape[0])

    qown[:, 0] = flipped(q_ref)
    g_t = flipped(g_ref)
    qown[:, 1] = g_t
    kown[:, 0] = flipped(k_ref)
    kown[:, 1] = flipped(v_ref)
    delta = jnp.sum(g_t.astype(F32) * flipped(o_ref).astype(F32), axis=1)
    lse2 = lse_ref[...] * LOG2E
    for j in range(ROW):
        sown[j, 0:PER] = lse2[j * PER:(j + 1) * PER]
        sown[j, PER:2 * PER] = delta[j * PER:(j + 1) * PER]

    pl.semaphore_wait(barrier, ROW - 1 + has_low.astype(jnp.int32) + has_high.astype(jnp.int32))

    def remote(src, dst, send, recv, target):
        return pltpu.make_async_remote_copy(
            src_ref=src, dst_ref=dst, send_sem=send, recv_sem=recv,
            device_id={"tok": target}, device_id_type=MESH,
        )

    def x_stat(d):
        to = (me + d) % ROW
        return remote(sown.at[to], sbuf.at[me + 2], ss.at[d], sr.at[d], mate(d))

    def x_q(d, h):
        to = (me + d) % ROW
        return remote(qown.at[to * PER + h], qbuf.at[me + 2, h], qs.at[d, h], qr.at[d, h], mate(d))

    def x_k(d, h):
        to = (me + d) % ROW
        return remote(kown.at[to * PER + h], kbuf.at[me, h], ks.at[d, h], kr.at[d, h], mate(d))

    def x_q_in(d, h):
        fr = (me + ROW - d) % ROW
        return remote(qown.at[0], qbuf.at[fr + 2, h], qs.at[d, h], qr.at[d, h], mate(d))

    def x_k_in(d, h):
        fr = (me + ROW - d) % ROW
        return remote(kown.at[0], kbuf.at[fr, h], ks.at[d, h], kr.at[d, h], mate(d))

    def x_stat_in(d):
        fr = (me + ROW - d) % ROW
        return remote(sown.at[0], sbuf.at[fr + 2], ss.at[d], sr.at[d], mate(d))

    order = (2, 1, 3)
    for d in order:
        x_stat(d).start()

    @pl.loop(0, PER)
    def _(h):
        for d in order:
            x_q(d, h).start()
        for d in order:
            x_k(d, h).start()

    @pl.loop(0, PER)
    def _(h):
        qbuf[me + 2, h] = qown[me * PER + h]
        kbuf[me, h] = kown[me * PER + h]

    sbuf[me + 2] = sown[me]

    @pl.when(jnp.logical_not(has_low))
    def _():
        dqr[0] = jnp.zeros(dqr.shape[1:], BF16)

    @pl.when(jnp.logical_not(has_high))
    def _():
        dqr[1] = jnp.zeros(dqr.shape[1:], BF16)

    def z_q(side, h):
        first, there = (2, 6) if side == 0 else (4, 0)
        target = tok - ROW if side == 0 else tok + ROW
        return remote(qbuf.at[pl.ds(first, 2), h], qbuf.at[pl.ds(there, 2), h],
                      zs.at[side, h], zr.at[1 - side, h], target)

    def z_q_in(side, h):
        here = 0 if side == 0 else 6
        target = tok - ROW if side == 0 else tok + ROW
        return remote(qbuf.at[pl.ds(here, 2), h], qbuf.at[pl.ds(here, 2), h],
                      zs.at[side, h], zr.at[side, h], target)

    def z_stat(side):
        first, there = (2, 6) if side == 0 else (4, 0)
        target = tok - ROW if side == 0 else tok + ROW
        return remote(sbuf.at[pl.ds(first, 2)], sbuf.at[pl.ds(there, 2)],
                      zss.at[side], zsr.at[1 - side], target)

    def z_stat_in(side):
        here = 0 if side == 0 else 6
        target = tok - ROW if side == 0 else tok + ROW
        return remote(sbuf.at[pl.ds(here, 2)], sbuf.at[pl.ds(here, 2)],
                      zss.at[side], zsr.at[side], target)

    def z_dq(side, h):
        target = tok - ROW if side == 0 else tok + ROW
        return remote(dqs.at[side, h], dqr.at[1 - side, h],
                      ds.at[side, h], dr.at[1 - side, h], target)

    def z_dq_in(side, h):
        target = tok - ROW if side == 0 else tok + ROW
        return remote(dqs.at[side, h], dqr.at[side, h],
                      ds.at[side, h], dr.at[side, h], target)

    def o_out(b, h):
        d = (b - me + ROW) % ROW
        return remote(obuf.at[b, h], orecv.at[me * PER + h],
                      os.at[d, h], orr.at[d, h], row * ROW + b)

    def o_in(d, h):
        fr = (me + ROW - d) % ROW
        return remote(obuf.at[0, h], orecv.at[fr * PER + h],
                      os.at[d, h], orr.at[d, h], mate(d))

    sides = ((0, has_low), (1, has_high))

    def sided(fn):
        for side, there in sides:
            @pl.when(there)
            def _():
                fn(side)

    for d in order:
        x_stat_in(d).wait_recv()
    sided(lambda side: z_stat(side).start())

    def task(c, slot, h, keys, values, keys_t):
        block = row * ROW + (slot - 2)
        flag = keep_ref[pl.ds(block, 1), c + 4 - slot:c + 5 - slot]
        gone = (1 - flag).astype(F32) * 1e30
        q_t, g_t = qbuf[slot, h, 0], qbuf[slot, h, 1]
        lse = sbuf[slot, pl.ds(h, 1), :] + gone
        delta = sbuf[slot, pl.ds(h + PER, 1), :]
        probs = jnp.exp2(dot_nn(keys, q_t) * (scale * LOG2E) - lse)
        grad = (probs * (dot_nn(values, g_t) - delta)).astype(BF16)
        return (
            dot_nn(keys_t, grad),
            dot_nt(q_t, grad),
            dot_nt(g_t, probs.astype(BF16)),
        )

    def run(h, work):
        seen = set()
        for c, slots, fresh in work:
            keys_t = kbuf[c, h, 0]
            keys = keys_t.T
            values = kbuf[c, h, 1].T
            dk = dv = None
            for slot in slots:
                tq, tk, tv = task(c, slot, h, keys, values, keys_t)
                dk = tk if dk is None else dk + tk
                dv = tv if dv is None else dv + tv
                if slot in seen:
                    dq[h, slot] += tq
                else:
                    dq[h, slot] = tq
                    seen.add(slot)
            if fresh:
                dkv[h, c, 0] = dk
                dkv[h, c, 1] = dv
            else:
                dkv[h, c, 0] += dk
                dkv[h, c, 1] += dv

    inner = ((0, (2, 3, 4), True), (1, (2, 3, 4, 5), True), (2, (2, 3, 4, 5), True), (3, (3, 4, 5), True))
    outer = (
        ((0, (0, 1), False), (1, (1,), False)),
        ((2, (6,), False), (3, (6, 7), False)),
    )

    def halo(side, h):
        z_q_in(side, h).wait_recv()
        run(h, outer[side])
        first = 0 if side == 0 else 6
        dqs[side, h] = (dq[h, pl.ds(first, 2)] * scale).astype(BF16)
        z_dq(side, h).start()

    def finish(h):
        sided(lambda side: z_dq_in(side, h).wait_recv())
        for b in range(ROW):
            total = dq[h, b + 2] * scale + dqr[b // 2, h, b % 2].astype(F32)
            obuf[b, h, 0] = total.astype(BF16)
            obuf[b, h, 1] = (dkv[h, b, 0] * scale).astype(BF16)
            obuf[b, h, 2] = dkv[h, b, 1].astype(BF16)

            @pl.when(b != me)
            def _():
                o_out(b, h).start()

            @pl.when(b == me)
            def _():
                orecv[me * PER + h] = obuf[b, h]

    @pl.loop(0, PER)
    def _(h):
        for d in order:
            x_q_in(d, h).wait_recv()
        sided(lambda side: z_q(side, h).start())
        for d in order:
            x_k_in(d, h).wait_recv()
        run(h, inner)

        @pl.when(h > 0)
        def _():
            finish(h - 1)

        @pl.when(h == 0)
        def _():
            sided(lambda side: z_stat_in(side).wait_recv())

        sided(lambda side: halo(side, h))

    finish(PER - 1)

    for d in order:
        x_stat(d).wait_send()
    sided(lambda side: z_stat(side).wait_send())

    @pl.loop(0, PER)
    def _(h):
        for d in order:
            x_q(d, h).wait_send()
            x_k(d, h).wait_send()
            o_in(d, h).wait_send()
            o_in(d, h).wait_recv()
        sided(lambda side: z_q(side, h).wait_send())
        sided(lambda side: z_dq(side, h).wait_send())


def unpack(packed_ref, *outs):
    for i, out in enumerate(outs):
        out[...] = packed_ref[:, i].reshape(out.shape[1], out.shape[0]).T


def per_device(count, query_rows, key_rows, value_rows, out_rows, grad_out, normalizer, keep_tasks):
    block, width = query_rows.shape
    dim = width // HEADS
    vmem = pl.BlockSpec(memory_space=pltpu.VMEM)
    dma = pltpu.SemaphoreType.DMA
    packed = pl.pallas_call(
        functools.partial(kernel, count),
        out_shape=jax.ShapeDtypeStruct((HEADS, 3, dim, block), BF16),
        in_specs=[vmem] * 7,
        out_specs=vmem,
        scratch_shapes=[
            pltpu.VMEM((HEADS, 2, dim, block), BF16),
            pltpu.VMEM((HEADS, 2, dim, block), BF16),
            pltpu.VMEM((ROW, 2 * PER, block), F32),
            pltpu.VMEM((ROW, PER, 2, dim, block), BF16),
            pltpu.VMEM((ROW + 4, PER, 2, dim, block), BF16),
            pltpu.VMEM((ROW + 4, 2 * PER, block), F32),
            pltpu.VMEM((PER, ROW + 4, dim, block), F32),
            pltpu.VMEM((PER, ROW, 2, dim, block), F32),
            pltpu.VMEM((2, PER, 2, dim, block), BF16),
            pltpu.VMEM((2, PER, 2, dim, block), BF16),
            pltpu.VMEM((ROW, PER, 3, dim, block), BF16),
            dma((ROW, PER)), dma((ROW, PER)),
            dma((ROW, PER)), dma((ROW, PER)),
            dma((ROW,)), dma((ROW,)),
            dma((2, PER)), dma((2, PER)),
            dma((2,)), dma((2,)),
            dma((2, PER)), dma((2, PER)),
            dma((ROW, PER)), dma((ROW, PER)),
        ],
        compiler_params=pltpu.CompilerParams(
            collective_id=0, has_side_effects=True, vmem_limit_bytes=60 * 1024 * 1024
        ),
    )(query_rows, key_rows, value_rows, out_rows, grad_out, normalizer, keep_tasks)
    return pl.pallas_call(
        unpack,
        out_shape=[jax.ShapeDtypeStruct((block, width), BF16)] * 3,
        in_specs=[vmem],
        out_specs=[vmem] * 3,
    )(packed)


def solution(mesh):
    rows = P(("groups", "tok"), None)
    return jax.shard_map(
        functools.partial(per_device, mesh.shape["tok"]),
        mesh=mesh,
        in_specs=(rows,) * 5 + (P(None, ("groups", "tok")), P("groups", None)),
        out_specs=(rows,) * 3,
        check_vma=False,
    )
```

```python
import functools

import jax
import jax.numpy as jnp
from jax import lax
from jax.experimental import pallas as pl
from jax.experimental.pallas import tpu as pltpu
from jax.sharding import PartitionSpec as P

HEADS = 16
ROW = 4
PER = HEADS // ROW
LOG2E = 1.4426950408889634
MESH = pl.DeviceIdType.MESH
F32 = jnp.float32
BF16 = jnp.bfloat16


def dot_nn(a, b):
    return lax.dot_general(a, b, (((1,), (0,)), ((), ())), preferred_element_type=F32)


def dot_nt(a, b):
    return lax.dot_general(a, b, (((1,), (1,)), ((), ())), preferred_element_type=F32)


def kernel(
    count, q_ref, k_ref, v_ref, o_ref, g_ref, lse_ref, keep_ref,
    orecv,
    kown, qown, sown, kbuf, qbuf, sbuf, dq, dkv, dqs, dqr, obuf,
    ks, kr, qs, qr, ss, sr, zs, zr, zss, zsr, ds, dr, os, orr,
):
    tok = lax.axis_index("tok")
    row, me = tok // ROW, tok % ROW
    rows = count // ROW
    has_low, has_high = row > 0, row < rows - 1
    width = q_ref.shape[1]
    dim = width // HEADS
    scale = dim ** -0.5

    barrier = pltpu.get_barrier_semaphore()

    def greet(target):
        pl.semaphore_signal(barrier, inc=1, device_id={"tok": target}, device_id_type=MESH)

    def mate(d):
        return row * ROW + (me + d) % ROW

    for d in range(1, ROW):
        greet(mate(d))

    @pl.when(has_low)
    def _():
        greet(tok - ROW)

    @pl.when(has_high)
    def _():
        greet(tok + ROW)

    def flipped(ref):
        return ref[...].T.reshape(HEADS, dim, ref.shape[0])

    qown[:, 0] = flipped(q_ref)
    g_t = flipped(g_ref)
    qown[:, 1] = g_t
    kown[:, 0] = flipped(k_ref)
    kown[:, 1] = flipped(v_ref)
    delta = jnp.sum(g_t.astype(F32) * flipped(o_ref).astype(F32), axis=1)
    lse2 = lse_ref[...] * LOG2E
    for j in range(ROW):
        sown[j, 0:PER] = lse2[j * PER:(j + 1) * PER]
        sown[j, PER:2 * PER] = delta[j * PER:(j + 1) * PER]

    pl.semaphore_wait(barrier, ROW - 1 + has_low.astype(jnp.int32) + has_high.astype(jnp.int32))

    def remote(src, dst, send, recv, target):
        return pltpu.make_async_remote_copy(
            src_ref=src, dst_ref=dst, send_sem=send, recv_sem=recv,
            device_id={"tok": target}, device_id_type=MESH,
        )

    def x_stat(d):
        to = (me + d) % ROW
        return remote(sown.at[to], sbuf.at[me + 2], ss.at[d], sr.at[d], mate(d))

    def x_q(d, h):
        to = (me + d) % ROW
        return remote(qown.at[to * PER + h], qbuf.at[me + 2, h], qs.at[d, h], qr.at[d, h], mate(d))

    def x_k(d, h):
        to = (me + d) % ROW
        return remote(kown.at[to * PER + h], kbuf.at[me, h], ks.at[d, h], kr.at[d, h], mate(d))

    def x_q_in(d, h):
        fr = (me + ROW - d) % ROW
        return remote(qown.at[0], qbuf.at[fr + 2, h], qs.at[d, h], qr.at[d, h], mate(d))

    def x_k_in(d, h):
        fr = (me + ROW - d) % ROW
        return remote(kown.at[0], kbuf.at[fr, h], ks.at[d, h], kr.at[d, h], mate(d))

    def x_stat_in(d):
        fr = (me + ROW - d) % ROW
        return remote(sown.at[0], sbuf.at[fr + 2], ss.at[d], sr.at[d], mate(d))

    order = (2, 1, 3)
    for d in order:
        x_stat(d).start()

    @pl.loop(0, PER)
    def _(h):
        for d in order:
            x_q(d, h).start()
        for d in order:
            x_k(d, h).start()

    @pl.loop(0, PER)
    def _(h):
        qbuf[me + 2, h] = qown[me * PER + h]
        kbuf[me, h] = kown[me * PER + h]

    sbuf[me + 2] = sown[me]

    @pl.when(jnp.logical_not(has_low))
    def _():
        dqr[0] = jnp.zeros(dqr.shape[1:], BF16)

    @pl.when(jnp.logical_not(has_high))
    def _():
        dqr[1] = jnp.zeros(dqr.shape[1:], BF16)

    def z_q(side, h):
        first, there = (2, 6) if side == 0 else (4, 0)
        target = tok - ROW if side == 0 else tok + ROW
        return remote(qbuf.at[pl.ds(first, 2), h], qbuf.at[pl.ds(there, 2), h],
                      zs.at[side, h], zr.at[1 - side, h], target)

    def z_q_in(side, h):
        here = 0 if side == 0 else 6
        target = tok - ROW if side == 0 else tok + ROW
        return remote(qbuf.at[pl.ds(here, 2), h], qbuf.at[pl.ds(here, 2), h],
                      zs.at[side, h], zr.at[side, h], target)

    def z_stat(side):
        first, there = (2, 6) if side == 0 else (4, 0)
        target = tok - ROW if side == 0 else tok + ROW
        return remote(sbuf.at[pl.ds(first, 2)], sbuf.at[pl.ds(there, 2)],
                      zss.at[side], zsr.at[1 - side], target)

    def z_stat_in(side):
        here = 0 if side == 0 else 6
        target = tok - ROW if side == 0 else tok + ROW
        return remote(sbuf.at[pl.ds(here, 2)], sbuf.at[pl.ds(here, 2)],
                      zss.at[side], zsr.at[side], target)

    def z_dq(side, h):
        target = tok - ROW if side == 0 else tok + ROW
        return remote(dqs.at[side, h], dqr.at[1 - side, h],
                      ds.at[side, h], dr.at[1 - side, h], target)

    def z_dq_in(side, h):
        target = tok - ROW if side == 0 else tok + ROW
        return remote(dqs.at[side, h], dqr.at[side, h],
                      ds.at[side, h], dr.at[side, h], target)

    def o_out(b, h):
        d = (b - me + ROW) % ROW
        return remote(obuf.at[b, h], orecv.at[me * PER + h],
                      os.at[d, h], orr.at[d, h], row * ROW + b)

    def o_in(d, h):
        fr = (me + ROW - d) % ROW
        return remote(obuf.at[0, h], orecv.at[fr * PER + h],
                      os.at[d, h], orr.at[d, h], mate(d))

    sides = ((0, has_low), (1, has_high))

    def sided(fn):
        for side, there in sides:
            @pl.when(there)
            def _():
                fn(side)

    for d in order:
        x_stat_in(d).wait_recv()
    sided(lambda side: z_stat(side).start())

    def task(c, slot, h, keys, values, keys_t):
        block = row * ROW + (slot - 2)
        flag = keep_ref[pl.ds(block, 1), c + 4 - slot:c + 5 - slot]
        gone = (1 - flag).astype(F32) * 1e30
        q_t, g_t = qbuf[slot, h, 0], qbuf[slot, h, 1]
        lse = sbuf[slot, pl.ds(h, 1), :] + gone
        delta = sbuf[slot, pl.ds(h + PER, 1), :]
        probs = jnp.exp2(dot_nn(keys, q_t) * (scale * LOG2E) - lse)
        grad = (probs * (dot_nn(values, g_t) - delta)).astype(BF16)
        return q_t, g_t, grad, probs.astype(BF16)

    def run(h, work):
        pieces = {}
        for c, slots, fresh in work:
            keys_t = kbuf[c, h, 0]
            keys = keys_t.T
            values = kbuf[c, h, 1].T
            parts = [task(c, slot, h, keys, values, keys_t) for slot in slots]
            q_all, g_all, grads, lows = [jnp.concatenate([p[i] for p in parts], axis=1) for i in range(4)]
            dk, dv = dot_nt(q_all, grads), dot_nt(g_all, lows)
            for slot, p in zip(slots, parts):
                pieces.setdefault(slot, []).append((keys_t, p[2]))
            if fresh:
                dkv[h, c, 0] = dk
                dkv[h, c, 1] = dv
            else:
                dkv[h, c, 0] += dk
                dkv[h, c, 1] += dv
        for slot, terms in pieces.items():
            dq[h, slot] = dot_nn(
                jnp.concatenate([t[0] for t in terms], axis=1),
                jnp.concatenate([t[1] for t in terms], axis=0),
            )

    inner = ((0, (2, 3, 4), True), (1, (2, 3, 4, 5), True), (2, (2, 3, 4, 5), True), (3, (3, 4, 5), True))
    outer = (
        ((0, (0, 1), False), (1, (1,), False)),
        ((2, (6,), False), (3, (6, 7), False)),
    )

    def halo(side, h):
        z_q_in(side, h).wait_recv()
        run(h, outer[side])
        first = 0 if side == 0 else 6
        dqs[side, h] = (dq[h, pl.ds(first, 2)] * scale).astype(BF16)
        z_dq(side, h).start()

    def finish(h):
        sided(lambda side: z_dq_in(side, h).wait_recv())
        for b in range(ROW):
            total = dq[h, b + 2] * scale + dqr[b // 2, h, b % 2].astype(F32)
            obuf[b, h, 0] = total.astype(BF16)
            obuf[b, h, 1] = (dkv[h, b, 0] * scale).astype(BF16)
            obuf[b, h, 2] = dkv[h, b, 1].astype(BF16)

            @pl.when(b != me)
            def _():
                o_out(b, h).start()

            @pl.when(b == me)
            def _():
                orecv[me * PER + h] = obuf[b, h]

    @pl.loop(0, PER)
    def _(h):
        for d in order:
            x_q_in(d, h).wait_recv()
        sided(lambda side: z_q(side, h).start())
        for d in order:
            x_k_in(d, h).wait_recv()
        run(h, inner)

        @pl.when(h > 0)
        def _():
            finish(h - 1)

        @pl.when(h == 0)
        def _():
            sided(lambda side: z_stat_in(side).wait_recv())

        sided(lambda side: halo(side, h))

    finish(PER - 1)

    for d in order:
        x_stat(d).wait_send()
    sided(lambda side: z_stat(side).wait_send())

    @pl.loop(0, PER)
    def _(h):
        for d in order:
            x_q(d, h).wait_send()
            x_k(d, h).wait_send()
            o_in(d, h).wait_send()
            o_in(d, h).wait_recv()
        sided(lambda side: z_q(side, h).wait_send())
        sided(lambda side: z_dq(side, h).wait_send())


def unpack(packed_ref, *outs):
    for i, out in enumerate(outs):
        out[...] = packed_ref[:, i].reshape(out.shape[1], out.shape[0]).T


def per_device(count, query_rows, key_rows, value_rows, out_rows, grad_out, normalizer, keep_tasks):
    block, width = query_rows.shape
    dim = width // HEADS
    vmem = pl.BlockSpec(memory_space=pltpu.VMEM)
    dma = pltpu.SemaphoreType.DMA
    packed = pl.pallas_call(
        functools.partial(kernel, count),
        out_shape=jax.ShapeDtypeStruct((HEADS, 3, dim, block), BF16),
        in_specs=[vmem] * 7,
        out_specs=vmem,
        scratch_shapes=[
            pltpu.VMEM((HEADS, 2, dim, block), BF16),
            pltpu.VMEM((HEADS, 2, dim, block), BF16),
            pltpu.VMEM((ROW, 2 * PER, block), F32),
            pltpu.VMEM((ROW, PER, 2, dim, block), BF16),
            pltpu.VMEM((ROW + 4, PER, 2, dim, block), BF16),
            pltpu.VMEM((ROW + 4, 2 * PER, block), F32),
            pltpu.VMEM((PER, ROW + 4, dim, block), F32),
            pltpu.VMEM((PER, ROW, 2, dim, block), F32),
            pltpu.VMEM((2, PER, 2, dim, block), BF16),
            pltpu.VMEM((2, PER, 2, dim, block), BF16),
            pltpu.VMEM((ROW, PER, 3, dim, block), BF16),
            dma((ROW, PER)), dma((ROW, PER)),
            dma((ROW, PER)), dma((ROW, PER)),
            dma((ROW,)), dma((ROW,)),
            dma((2, PER)), dma((2, PER)),
            dma((2,)), dma((2,)),
            dma((2, PER)), dma((2, PER)),
            dma((ROW, PER)), dma((ROW, PER)),
        ],
        compiler_params=pltpu.CompilerParams(
            collective_id=0, has_side_effects=True, vmem_limit_bytes=60 * 1024 * 1024
        ),
    )(query_rows, key_rows, value_rows, out_rows, grad_out, normalizer, keep_tasks)
    return pl.pallas_call(
        unpack,
        out_shape=[jax.ShapeDtypeStruct((block, width), BF16)] * 3,
        in_specs=[vmem],
        out_specs=[vmem] * 3,
    )(packed)


def solution(mesh):
    rows = P(("groups", "tok"), None)
    return jax.shard_map(
        functools.partial(per_device, mesh.shape["tok"]),
        mesh=mesh,
        in_specs=(rows,) * 5 + (P(None, ("groups", "tok")), P("groups", None)),
        out_specs=(rows,) * 3,
        check_vma=False,
    )
```
